32 devices in a mesh: grp: 2 (over y), row: 4 (over x, core), col: 4 (over z).
Axes of the slice: x: 2, y: 2, z: 4, core: 2. Of those that a mesh axis runs over, the one named last changes fastest.
Arguments:
- sigma_anc: float32 [1536, 768], P(('grp', 'row'), 'col'), parts along dimension 0, may hold values from -3 to 23, as said below
- anc_factor: float32 [1536, 2, 512], P(('grp', 'row', 'col')), parts along dimension 0, may hold values from -0.625 to 0.625
- diag_inverse: float32 [4, 512, 512], P('grp', None, 'row'), parts along dimension 0, may hold values from -0.6 to 1.5, as said below
- pattern: int32 [2, 6], replicated, may hold values from 0 to 1, as said below
Outputs:
- sel_off: float32 [1536, 2, 512], P(('grp', 'row', 'col')), parts along dimension 0
- sel_diag: float32 [4, 512, 512], P('grp'), parts along dimension 0
The draws below stay inside these ranges and needn't reach their ends.
There are 2 independent parts, one for each index of `grp`. The reference program is written for one: setup_inputs(seed, part) draws one part's arguments, and reference() takes and returns one part's arrays. A program takes and returns all parts, laid end to end along the dimension named above; an argument that names none is the same for every part. Nothing has to cross between parts.
Inputs may be any that keep to these rules, and one draw needn't show every extreme that they name: `pattern`: each supernode's present row blocks are a run of consecutive blocks, wrapping around the end, of at least 0 blocks, at most 3, together with some scattered others. `sigma_anc`: symmetric and positive definite. `diag_inverse`: lower triangular, with diagonal entries between 0.5 and 1.5 and small entries below the diagonal.
All inputs are finite; a program needn't handle non-finite values.
Results may differ from the reference program's by a relative error of at most 0.00013.
Values sent between devices are 32-bit elements; how exact they have to be, the bound alone decides.
No kernel may reach another device: no remote copies, remote signals or barrier semaphores. Data moves between devices by JAX's collectives and lax.ppermute only.
A program may use at most 64 MiB of HBM per device.

```python
import math
import jax
import jax.numpy as jnp
from jax import lax

WID = 512
SUPERS = 2
BLK = 128
R = 768
NBLK = 6


def draw_sigma_anc(key, part):
    key = jax.random.fold_in(key, 11)
    key_noise, key_diag = jax.random.split(key, 2)
    noise = jax.random.normal(key_noise, (R, R), jnp.float32)
    matrix = (noise + jnp.transpose(noise)) * (0.3 / math.sqrt(R))
    diagonal = jax.random.uniform(key_diag, (R,), jnp.float32, 1.0, 2.0)
    matrix = matrix + jnp.diag(diagonal)
    return matrix


def draw_diag_inverse(key, part):
    key = jax.random.fold_in(key, 23)
    key_noise, key_diag = jax.random.split(key, 2)
    noise = jax.random.normal(key_noise, (SUPERS, WID, WID), jnp.float32) * (0.5 / math.sqrt(WID))
    lower = jnp.tril(noise, -1)
    diagonal = jax.random.uniform(key_diag, (SUPERS, WID), jnp.float32, 0.5, 1.5)
    identity = jnp.eye(WID, dtype=jnp.float32)
    return lower + diagonal[:, :, None] * identity[None, :, :]


def draw_pattern(key, part):
    key = jax.random.fold_in(key, 37)
    key_start, key_length, key_extra = jax.random.split(key, 3)
    first_block = jax.random.randint(key_start, (SUPERS, 1), 0, NBLK)
    run_length = jax.random.randint(key_length, (SUPERS, 1), max(1, NBLK // 8), NBLK // 2 + 1)
    positions = jnp.arange(NBLK, dtype=jnp.int32)[None, :]
    inside = (positions - first_block) % NBLK < run_length
    scattered = jax.random.randint(key_extra, (SUPERS, NBLK), 0, 8) == 0
    return jnp.where(inside | scattered, 1, 0).astype(jnp.int32)


def levels(stream_key, shape, cuts, smallest, top_value):
    gain = 1.0
    for position, blocks in cuts:
        heights = jax.random.uniform(jax.random.fold_in(jax.random.fold_in(stream_key, 6), position), (blocks,), jnp.float32, smallest / len(cuts), top_value / len(cuts))
        gain = gain * jnp.repeat(jnp.exp(heights), shape[position] // blocks).reshape((-1,) + (1,) * (len(shape) - 1 - position))
    return gain


def scatter_about(own_key, shape, width, bound, cuts=(), held_as=jnp.bfloat16):
    result = jax.random.normal(own_key, shape, jnp.float32) * width
    if len(cuts) > 0:
        result = levels(own_key, shape, cuts, -0.22, 0.18) * result
    return jnp.clip(result, min=-bound, max=bound).astype(held_as)


def setup_inputs(seed: int = 0, part: int = 0) -> dict:
    keys = jax.random.split(jax.random.key(seed), 5)
    part_keys = jax.random.split(jax.random.fold_in(keys[4], part), 5)
    return {
        "sigma_anc": draw_sigma_anc(jax.random.fold_in(jax.random.fold_in(keys[4], part), 71), part),
        "anc_factor": scatter_about(part_keys[1], (R, SUPERS, WID), (R // 8) ** -0.5, 0.625, ((0, 16),), jnp.float32),
        "diag_inverse": draw_diag_inverse(jax.random.fold_in(jax.random.fold_in(keys[4], part), 71), part),
        "pattern": draw_pattern(jax.random.fold_in(keys[4], 71), part),
    }


def reference(sigma_anc, anc_factor, diag_inverse, pattern):
    precise = lax.Precision.HIGHEST
    row_mask = jnp.repeat(pattern.astype(jnp.float32), BLK, axis=1)
    mask_rows = jnp.transpose(row_mask)[:, :, None]
    scaled = jnp.einsum("rsk,skj->rsj", anc_factor, diag_inverse, precision=precise) * mask_rows
    flattened = scaled.reshape(R, SUPERS * WID)
    product = jnp.dot(sigma_anc, flattened, precision=precise, preferred_element_type=jnp.float32)
    sel_off = -(product.reshape(R, SUPERS, WID) * mask_rows)
    first_term = jnp.einsum("skj,skl->sjl", diag_inverse, diag_inverse, precision=precise)
    second_term = jnp.einsum("rsj,rsl->sjl", scaled, sel_off, precision=precise)
    sel_diag = first_term - second_term
    return sel_off, sel_diag
```

```python
import jax
import jax.numpy as jnp
from jax import lax
from jax.sharding import PartitionSpec as P


def own_row_mask(pattern, rows_dev, position, total_rows):
    block_size = total_rows // pattern.shape[1]
    flat_mask = jnp.repeat(pattern.astype(jnp.float32), block_size, axis=1)
    return jnp.transpose(lax.dynamic_slice_in_dim(flat_mask, position * rows_dev, rows_dev, 1))[
        :, :, None
    ]


def reduce_body(sigma_anc, anc_factor, diag_inverse, pattern):
    precise = lax.Precision.HIGHEST
    rows_dev, supers, super_width = anc_factor.shape
    row_count = lax.axis_size("row")
    col_count = lax.axis_size("col")
    position = lax.axis_index("row") * col_count + lax.axis_index("col")
    device_total = row_count * col_count
    own_mask = own_row_mask(pattern, rows_dev, position, rows_dev * device_total)
    share = -(-super_width // device_total)
    masked_factor = anc_factor * own_mask
    flattened = masked_factor.reshape(rows_dev, -1)
    gathered = lax.all_gather(flattened, "row", axis=0, tiled=True)
    stacked = gathered.reshape(row_count, rows_dev, flattened.shape[1])
    turned = lax.all_to_all(stacked, "col", split_axis=0, concat_axis=1, tiled=True)
    column_block = turned.reshape(row_count * rows_dev, flattened.shape[1])
    summed_rows = lax.psum_scatter(
        jnp.dot(sigma_anc, column_block, precision=precise, preferred_element_type=jnp.float32),
        "col",
        scatter_dimension=0,
        tiled=True,
    )
    off_factor = -(summed_rows.reshape(masked_factor.shape) * own_mask)
    both_rows = jnp.concatenate([masked_factor, off_factor], axis=0)
    column_piece = lax.all_gather(diag_inverse, "row", axis=2, tiled=True)
    product = jnp.einsum("rsk,skj->rsj", both_rows, column_piece, precision=precise)
    own_rows = lax.dynamic_slice_in_dim(column_piece, position * share, share, 1)
    scaled = product[:rows_dev]
    sel_off = product[rows_dev:]
    diag_term = jnp.einsum("skj,skl->sjl", own_rows, own_rows, precision=precise)
    partial_value = diag_term - jnp.einsum("rsj,rsl->sjl", scaled, sel_off, precision=precise)
    sel_diag = lax.psum(partial_value, ("row", "col"))
    return (sel_off, sel_diag)


def swap(value, axis, bit):
    count = lax.axis_size(axis)
    return lax.ppermute(value, axis, [(i, i ^ bit) for i in range(count)])


def gather_body(sigma_anc, anc_factor, diag_inverse, pattern):
    high = lax.Precision.HIGH
    rows_dev, supers, width = anc_factor.shape
    row_count = lax.axis_size("row")
    col_count = lax.axis_size("col")
    cores = row_count // supers
    row = lax.axis_index("row")
    col = lax.axis_index("col")
    plane = row // cores
    core = row % cores
    block_rows = rows_dev * col_count
    own_mask = own_row_mask(pattern, rows_dev, row * col_count + col, block_rows * row_count)
    masked = jnp.swapaxes(anc_factor * own_mask, 0, 1)

    def other_plane(value):
        return swap(value, "row", cores)

    def other_core(value):
        return swap(value, "row", 1)

    def pick(value, index):
        return lax.dynamic_index_in_dim(value, index, 0, keepdims=False)

    mine = pick(masked, plane)
    partner = other_plane(pick(masked, 1 - plane))
    d_own = pick(diag_inverse, plane)
    d_partner = other_plane(pick(diag_inverse, 1 - plane))

    def along_col(value):
        far = swap(value, "col", 2)
        near = swap(value, "col", 1)
        last = swap(far, "col", 1)
        return [value, near, far, last]

    sig = along_col(sigma_anc)
    sig_partner = [other_plane(v) for v in sig]
    pieces = along_col(jnp.stack([mine, partner]))
    pieces_core = [other_core(v) for v in pieces]
    full = jnp.zeros((row_count, col_count, rows_dev, width), jnp.float32)
    for k in range(col_count):
        for c, group in ((0, pieces[k]), (1, pieces_core[k])):
            for p in range(supers):
                full = lax.dynamic_update_slice(
                    full, group[p][None, None], (row ^ (p * cores + c), col ^ k, 0, 0)
                )
    full = full.reshape(row_count, block_rows, width)
    ordered = jnp.concatenate([pick(full, col ^ k) for k in range(col_count)], axis=0)
    sig_rows = jnp.concatenate(
        [jnp.concatenate([a, b], axis=0) for a, b in zip(sig, sig_partner)], axis=1
    )
    weighted = jnp.dot(sig_rows, ordered, precision=high, preferred_element_type=jnp.float32)
    share = diag_inverse.shape[2]
    d_pair = jnp.stack([d_own, d_partner])
    d_pair_core = other_core(d_pair)
    dinv = jnp.zeros((width, width), jnp.float32)
    for c, group in ((0, d_pair), (1, d_pair_core)):
        for p in range(supers):
            dinv = lax.dynamic_update_slice(dinv, group[p], (0, (row ^ (p * cores + c)) * share))
    half_rows = jnp.concatenate([pick(full, row), pick(full, row ^ cores)], axis=0)
    scaled = jnp.dot(half_rows, dinv, precision=high)
    spread = jnp.dot(weighted, dinv, precision=high)
    d_half = lax.dynamic_slice_in_dim(dinv, core * (width // cores), width // cores, 0)
    contract = (((0,), (0,)), ((), ()))
    part = lax.dot_general(d_half, d_half, contract, precision=high) + lax.dot_general(
        scaled, spread, contract, precision=high
    )
    spread_blocks = spread.reshape(supers, col_count, rows_dev, width)
    kept = lax.dynamic_slice_in_dim(spread_blocks[0], col, 1, 0)[0]
    sent = lax.dynamic_slice_in_dim(spread_blocks[1], col, 1, 0)[0]
    got = other_plane(sent)
    first = plane == 0
    off = jnp.stack([jnp.where(first, kept, got), jnp.where(first, got, kept)], axis=1)
    sel_off = -(off * own_mask)
    half = width // cores
    halves = part.reshape(cores, half, width)
    own_half = pick(halves, core) + other_core(pick(halves, 1 - core))
    far_half = other_plane(own_half)
    both = jnp.stack([jnp.where(first, own_half, far_half), jnp.where(first, far_half, own_half)])
    both_core = other_core(both)
    low = core == 0
    sel_diag = jnp.concatenate(
        [jnp.where(low, both, both_core), jnp.where(low, both_core, both)], axis=1
    )
    return (sel_off, sel_diag)


def body(sigma_anc, anc_factor, diag_inverse, pattern):
    supers = anc_factor.shape[1]
    if lax.axis_size("row") == 2 * supers == 4 and lax.axis_size("col") == 4:
        return gather_body(sigma_anc, anc_factor, diag_inverse, pattern)
    return reduce_body(sigma_anc, anc_factor, diag_inverse, pattern)


def solution(mesh):
    return jax.shard_map(
        body,
        mesh=mesh,
        in_specs=(
            P(("grp", "row"), "col"),
            P(("grp", "row", "col"), None, None),
            P("grp", None, "row"),
            P(),
        ),
        out_specs=(P(("grp", "row", "col"), None, None), P("grp", None, None)),
        check_vma=False,
    )
```

```python
import functools

import jax
import jax.numpy as jnp
from jax import lax
from jax.experimental import pallas as pl
from jax.experimental.pallas import tpu as pltpu
from jax.sharding import PartitionSpec as P


def own_row_mask(pattern, rows_dev, position, total_rows):
    block_size = total_rows // pattern.shape[1]
    flat_mask = jnp.repeat(pattern.astype(jnp.float32), block_size, axis=1)
    return jnp.transpose(lax.dynamic_slice_in_dim(flat_mask, position * rows_dev, rows_dev, 1))[
        :, :, None
    ]


def reduce_body(sigma_anc, anc_factor, diag_inverse, pattern):
    precise = lax.Precision.HIGHEST
    rows_dev, _, super_width = anc_factor.shape
    row_count = lax.axis_size("row")
    col_count = lax.axis_size("col")
    position = lax.axis_index("row") * col_count + lax.axis_index("col")
    device_total = row_count * col_count
    own_mask = own_row_mask(pattern, rows_dev, position, rows_dev * device_total)
    share = -(-super_width // device_total)
    masked_factor = anc_factor * own_mask
    flattened = masked_factor.reshape(rows_dev, -1)
    gathered = lax.all_gather(flattened, "row", axis=0, tiled=True)
    stacked = gathered.reshape(row_count, rows_dev, flattened.shape[1])
    turned = lax.all_to_all(stacked, "col", split_axis=0, concat_axis=1, tiled=True)
    column_block = turned.reshape(row_count * rows_dev, flattened.shape[1])
    summed_rows = lax.psum_scatter(
        jnp.dot(sigma_anc, column_block, precision=precise, preferred_element_type=jnp.float32),
        "col",
        scatter_dimension=0,
        tiled=True,
    )
    off_factor = -(summed_rows.reshape(masked_factor.shape) * own_mask)
    both_rows = jnp.concatenate([masked_factor, off_factor], axis=0)
    column_piece = lax.all_gather(diag_inverse, "row", axis=2, tiled=True)
    product = jnp.einsum("rsk,skj->rsj", both_rows, column_piece, precision=precise)
    own_rows = lax.dynamic_slice_in_dim(column_piece, position * share, share, 1)
    scaled = product[:rows_dev]
    sel_off = product[rows_dev:]
    diag_term = jnp.einsum("skj,skl->sjl", own_rows, own_rows, precision=precise)
    partial_value = diag_term - jnp.einsum("rsj,rsl->sjl", scaled, sel_off, precision=precise)
    sel_diag = lax.psum(partial_value, ("row", "col"))
    return (sel_off, sel_diag)


def swap(value, axis, bit):
    count = lax.axis_size(axis)
    return lax.ppermute(value, axis, [(i, i ^ bit) for i in range(count)])


def unique_blocks(value, core, tile):
    base = core * 2 * tile
    blocks = []
    for i, j in ((0, 0), (0, 1), (1, 1)):
        blocks.append(
            lax.dynamic_slice(value, (base + i * tile, base + j * tile), (tile, tile))
        )
    for i in range(2):
        across = jnp.where(core == 0, 2 + i, 1 - i)
        blocks.append(
            lax.dynamic_slice(value, (base + i * tile, across * tile), (tile, tile))
        )
    return jnp.concatenate(blocks, axis=0)


def lay_out(tile, place_ref, mine_ref, other_ref, *refs):
    out_ref, square, sem = refs[-3:]
    for step, source in ((0, mine_ref), (1, other_ref)):
        core = lax.rem(place_ref[1] + step, 2)
        base = pl.multiple_of(core * (2 * tile), 2 * tile)

        def put(row, column, block):
            square[
                pl.ds(pl.multiple_of(row, tile), tile), pl.ds(pl.multiple_of(column, tile), tile)
            ] = block

        def block(i):
            return source[pl.ds(i * tile, tile), :]

        put(base, base, block(0))
        upper = block(1)
        put(base, base + tile, upper)
        put(base + tile, base, upper.T)
        put(base + tile, base + tile, block(2))
        for i in range(2):
            across = jnp.where(core == 0, 2 + i, 1 - i) * tile
            side = block(3 + i)
            put(base + i * tile, across, side)
            put(across, base + i * tile, side.T)
    copy = pltpu.make_async_copy(square, out_ref.at[place_ref[0]], sem)
    copy.start()
    copy.wait()


def place_square(supers, width, index, core, mine, other, target=None):
    tile = width // 4
    place = jnp.stack([index, core]).astype(jnp.int32)
    args = [place, mine, other] + ([] if target is None else [target])
    return pl.pallas_call(
        functools.partial(lay_out, tile),
        out_shape=jax.ShapeDtypeStruct((supers, width, width), jnp.float32),
        in_specs=[
            pl.BlockSpec(memory_space=pltpu.SMEM),
            pl.BlockSpec(memory_space=pltpu.VMEM),
            pl.BlockSpec(memory_space=pltpu.VMEM),
        ]
        + ([] if target is None else [pl.BlockSpec(memory_space=pl.ANY)]),
        out_specs=pl.BlockSpec(memory_space=pl.ANY),
        scratch_shapes=[pltpu.VMEM((width, width), jnp.float32), pltpu.SemaphoreType.DMA],
        input_output_aliases={} if target is None else {3: 0},
        cost_estimate=pl.CostEstimate(
            flops=0, transcendentals=0, bytes_accessed=2 * 4 * width * width
        ),
        compiler_params=pltpu.CompilerParams(vmem_limit_bytes=8 * 4 * width * width),
        name="lay_out_square",
    )(*args)


def gather_body(sigma_anc, anc_factor, diag_inverse, pattern):
    high = lax.Precision.HIGH
    rows_dev, supers, width = anc_factor.shape
    row_count = lax.axis_size("row")
    col_count = lax.axis_size("col")
    cores = row_count // supers
    row = lax.axis_index("row")
    col = lax.axis_index("col")
    plane = row // cores
    core = row % cores
    block_rows = rows_dev * col_count
    own_mask = own_row_mask(pattern, rows_dev, row * col_count + col, block_rows * row_count)
    masked = jnp.swapaxes(anc_factor * own_mask, 0, 1)

    def other_plane(value):
        return swap(value, "row", cores)

    def other_core(value):
        return swap(value, "row", 1)

    def pick(value, index):
        return lax.dynamic_index_in_dim(value, index, 0, keepdims=False)

    mine = pick(masked, plane)
    theirs, sigma_own = lax.optimization_barrier((pick(masked, 1 - plane), sigma_anc))
    partner = other_plane(theirs)
    d_own = pick(diag_inverse, plane)
    d_partner = other_plane(pick(diag_inverse, 1 - plane))

    def along_col(value):
        far = swap(value, "col", 2)
        near = swap(value, "col", 1)
        last = swap(far, "col", 1)
        return [value, near, far, last]

    sig = along_col(sigma_own)
    sig_partner = []
    for k in range(col_count):
        sig_partner.append(other_plane(sig[k]))
    pieces = along_col(jnp.stack([mine, partner]))
    pieces_core = []
    for k in range(col_count):
        pieces_core.append(other_core(pieces[k]))
    half_full = jnp.zeros((supers, col_count, rows_dev, width), jnp.float32)
    rest_full = half_full
    for k in range(col_count):
        for p in range(supers):
            at = (plane ^ p, col ^ k, 0, 0)
            half_full = lax.dynamic_update_slice(half_full, pieces[k][p][None, None], at)
            rest_full = lax.dynamic_update_slice(rest_full, pieces_core[k][p][None, None], at)
    half_full = half_full.reshape(supers, block_rows, width)
    rest_full = rest_full.reshape(supers, block_rows, width)
    own_first = core == 0
    even = jnp.where(own_first, half_full, rest_full)
    odd = jnp.where(own_first, rest_full, half_full)
    full = jnp.stack([even, odd], axis=1).reshape(row_count, block_rows, width)
    ordered = jnp.concatenate([pick(full, col ^ k) for k in range(col_count)], axis=0)
    sig_rows = jnp.concatenate(
        [jnp.concatenate([a, b], axis=0) for a, b in zip(sig, sig_partner)], axis=1
    )
    weighted = jnp.dot(sig_rows, ordered, precision=high, preferred_element_type=jnp.float32)
    share = diag_inverse.shape[2]
    d_pair = jnp.stack([d_own, d_partner])
    d_pair_core = other_core(d_pair)
    dinv = jnp.zeros((width, width), jnp.float32)
    for c, group in ((0, d_pair), (1, d_pair_core)):
        for p in range(supers):
            dinv = lax.dynamic_update_slice(dinv, group[p], (0, (row ^ (p * cores + c)) * share))
    half_rows = jnp.concatenate([pick(half_full, plane), pick(half_full, 1 - plane)], axis=0)
    scaled = jnp.dot(half_rows, dinv, precision=high)
    d_half = lax.dynamic_slice_in_dim(dinv, core * (width // cores), width // cores, 0)
    contract = (((0,), (0,)), ((), ()))
    gram = lax.dot_general(d_half, d_half, contract, precision=high)
    gram = lax.optimization_barrier(gram)
    spread = jnp.dot(weighted, dinv, precision=high)
    spread_blocks = spread.reshape(supers, col_count, rows_dev, width)
    kept = lax.dynamic_slice_in_dim(spread_blocks[0], col, 1, 0)[0]
    sent = lax.dynamic_slice_in_dim(spread_blocks[1], col, 1, 0)[0]
    sent, spread = lax.optimization_barrier((sent, spread))
    got = other_plane(sent)
    first = plane == 0
    off = jnp.stack([jnp.where(first, kept, got), jnp.where(first, got, kept)], axis=1)
    sel_off = -(off * own_mask)
    part = gram + lax.dot_general(scaled, spread, contract, precision=high)
    tile = width // 4
    finished = unique_blocks(part, core, tile) + other_core(unique_blocks(part, 1 - core, tile))
    far_finished = other_plane(finished)
    finished_core = other_core(finished)
    far_core = other_core(far_finished)
    square = place_square(supers, width, plane, core, finished, finished_core)
    sel_diag = place_square(supers, width, 1 - plane, core, far_finished, far_core, square)
    return (sel_off, sel_diag)


def gather_fits(row_count, col_count, supers):
    return row_count == 2 * supers == 4 and col_count == 4


def body(sigma_anc, anc_factor, diag_inverse, pattern):
    supers = anc_factor.shape[1]
    if gather_fits(lax.axis_size("row"), lax.axis_size("col"), supers):
        return gather_body(sigma_anc, anc_factor, diag_inverse, pattern)
    return reduce_body(sigma_anc, anc_factor, diag_inverse, pattern)


def solution(mesh):
    return jax.shard_map(
        body,
        mesh=mesh,
        in_specs=(
            P(("grp", "row"), "col"),
            P(("grp", "row", "col"), None, None),
            P("grp", None, "row"),
            P(),
        ),
        out_specs=(P(("grp", "row", "col"), None, None), P("grp", None, None)),
        check_vma=False,
    )
```

```python
import functools

import jax
import jax.numpy as jnp
from jax import lax
from jax.experimental import pallas as pl
from jax.experimental.pallas import tpu as pltpu
from jax.sharding import PartitionSpec as P


def own_row_mask(pattern, rows_dev, position, total_rows):
    block_size = total_rows // pattern.shape[1]
    flat_mask = jnp.repeat(pattern.astype(jnp.float32), block_size, axis=1)
    return jnp.transpose(lax.dynamic_slice_in_dim(flat_mask, position * rows_dev, rows_dev, 1))[
        :, :, None
    ]


def reduce_body(sigma_anc, anc_factor, diag_inverse, pattern):
    precise = lax.Precision.HIGHEST
    rows_dev, _, super_width = anc_factor.shape
    row_count = lax.axis_size("row")
    col_count = lax.axis_size("col")
    position = lax.axis_index("row") * col_count + lax.axis_index("col")
    device_total = row_count * col_count
    own_mask = own_row_mask(pattern, rows_dev, position, rows_dev * device_total)
    share = -(-super_width // device_total)
    masked_factor = anc_factor * own_mask
    flattened = masked_factor.reshape(rows_dev, -1)
    gathered = lax.all_gather(flattened, "row", axis=0, tiled=True)
    stacked = gathered.reshape(row_count, rows_dev, flattened.shape[1])
    turned = lax.all_to_all(stacked, "col", split_axis=0, concat_axis=1, tiled=True)
    column_block = turned.reshape(row_count * rows_dev, flattened.shape[1])
    summed_rows = lax.psum_scatter(
        jnp.dot(sigma_anc, column_block, precision=precise, preferred_element_type=jnp.float32),
        "col",
        scatter_dimension=0,
        tiled=True,
    )
    off_factor = -(summed_rows.reshape(masked_factor.shape) * own_mask)
    both_rows = jnp.concatenate([masked_factor, off_factor], axis=0)
    column_piece = lax.all_gather(diag_inverse, "row", axis=2, tiled=True)
    product = jnp.einsum("rsk,skj->rsj", both_rows, column_piece, precision=precise)
    own_rows = lax.dynamic_slice_in_dim(column_piece, position * share, share, 1)
    scaled = product[:rows_dev]
    sel_off = product[rows_dev:]
    diag_term = jnp.einsum("skj,skl->sjl", own_rows, own_rows, precision=precise)
    partial_value = diag_term - jnp.einsum("rsj,rsl->sjl", scaled, sel_off, precision=precise)
    sel_diag = lax.psum(partial_value, ("row", "col"))
    return (sel_off, sel_diag)


def swap(value, axis, bit):
    count = lax.axis_size(axis)
    return lax.ppermute(value, axis, [(i, i ^ bit) for i in range(count)])


def unique_blocks(band, core, tile):
    base = core * 2 * tile
    blocks = []
    for i, j in ((0, 0), (0, 1), (1, 1)):
        blocks.append(lax.dynamic_slice(band, (i * tile, base + j * tile), (tile, tile)))
    for i in range(2):
        across = jnp.where(core == 0, 2 + i, 1 - i)
        blocks.append(lax.dynamic_slice(band, (i * tile, across * tile), (tile, tile)))
    return jnp.concatenate(blocks, axis=0)


def lay_out(tile, sources, place_ref, *refs):
    out_ref, turned, sems = refs[-3:]
    copies = []
    for step in range(sources):
        source = refs[step]
        core = lax.rem(place_ref[1] + step, 2)
        base = core * (2 * tile)

        def put(value, row, column):
            row, column = pl.multiple_of(row, tile), pl.multiple_of(column, tile)
            copies.append(
                pltpu.make_async_copy(
                    value,
                    out_ref.at[place_ref[0], pl.ds(row, tile), pl.ds(column, tile)],
                    sems.at[len(copies)],
                )
            )
            copies[-1].start()

        def block(i):
            return source.at[pl.ds(i * tile, tile), :]

        places = [(base, base + tile)]
        put(block(0), base, base)
        put(block(2), base + tile, base + tile)
        for i in range(2):
            places.append((base + i * tile, jnp.where(core == 0, 2 + i, 1 - i) * tile))
        for i, (block_id, (row, column)) in enumerate(zip((1, 3, 4), places)):
            put(block(block_id), row, column)
            turned[3 * step + i] = block(block_id)[...].T
            put(turned.at[3 * step + i], column, row)
    for copy in copies:
        copy.wait()


def place_square(supers, width, index, core, parts, target=None):
    tile = width // 4
    place = jnp.stack([index, core]).astype(jnp.int32)
    args = [place, *parts] + ([] if target is None else [target])
    return pl.pallas_call(
        functools.partial(lay_out, tile, len(parts)),
        out_shape=jax.ShapeDtypeStruct((supers, width, width), jnp.float32),
        in_specs=[pl.BlockSpec(memory_space=pltpu.SMEM)]
        + [pl.BlockSpec(memory_space=pltpu.VMEM)] * len(parts)
        + ([] if target is None else [pl.BlockSpec(memory_space=pl.ANY)]),
        out_specs=pl.BlockSpec(memory_space=pl.ANY),
        scratch_shapes=[
            pltpu.VMEM((3 * len(parts), tile, tile), jnp.float32),
            pltpu.SemaphoreType.DMA((8 * len(parts),)),
        ],
        input_output_aliases={} if target is None else {1 + len(parts): 0},
        cost_estimate=pl.CostEstimate(
            flops=0, transcendentals=0, bytes_accessed=2 * 4 * width * width
        ),
        compiler_params=pltpu.CompilerParams(vmem_limit_bytes=8 * 4 * width * width),
        name="lay_out_square",
    )(*args)


def join_rows(mask_ref, first_ref, second_ref, out_ref):
    out_ref[:, 0, :] = -(first_ref[...] * mask_ref[:, 0:1])
    out_ref[:, 1, :] = -(second_ref[...] * mask_ref[:, 1:2])


def gather_body(sigma_anc, anc_factor, diag_inverse, pattern):
    high = lax.Precision.HIGH
    rows_dev, supers, width = anc_factor.shape
    row_count = lax.axis_size("row")
    col_count = lax.axis_size("col")
    cores = row_count // supers
    row = lax.axis_index("row")
    col = lax.axis_index("col")
    plane = row // cores
    core = row % cores
    first = plane == 0
    block_rows = rows_dev * col_count
    total_rows = block_rows * row_count
    tile = width // 4
    half = width // cores

    def other_plane(value):
        return swap(value, "row", cores)

    def other_core(value):
        return swap(value, "row", 1)

    def pick(value, index):
        return lax.dynamic_index_in_dim(value, index, 0, keepdims=False)

    def along_col(value):
        far = swap(value, "col", 2)
        near = swap(value, "col", 1)
        last = swap(far, "col", 1)
        return [value, near, far, last]

    def at_super(value, index):
        return lax.dynamic_index_in_dim(value, index, 1, keepdims=False)

    theirs = at_super(anc_factor, 1 - plane)
    mine = at_super(anc_factor, plane)
    partner = other_plane(theirs)
    flat_mask = jnp.repeat(pattern.astype(jnp.float32), total_rows // pattern.shape[1], axis=1)

    def mask_at(block):
        return lax.dynamic_slice_in_dim(flat_mask, block * block_rows + col * rows_dev, rows_dev, 1)

    own_mask = jnp.transpose(mask_at(row))
    pair_mask = jnp.stack([pick(mask_at(row), plane), pick(mask_at(row ^ cores), plane)])
    masked = jnp.stack([mine, partner]) * pair_mask[:, :, None]
    pieces = along_col(masked)
    pieces_core = [other_core(pieces[k]) for k in range(col_count)]

    sig = along_col(sigma_anc)
    sig_partner = [other_plane(sig[k]) for k in range(col_count)]

    share = diag_inverse.shape[2]
    d_own = pick(diag_inverse, plane)
    d_partner = other_plane(pick(diag_inverse, 1 - plane))
    d_pair = jnp.stack([d_own, d_partner])
    d_pair_core = other_core(d_pair)
    dinv = jnp.zeros((width, width), jnp.float32)
    for c, group in ((0, d_pair), (1, d_pair_core)):
        for p in range(supers):
            dinv = lax.dynamic_update_slice(dinv, group[p], (0, (row ^ (p * cores + c)) * share))

    half_rows = jnp.zeros((supers, col_count, rows_dev, width), jnp.float32)
    ordered = jnp.zeros((row_count, col_count, rows_dev, width), jnp.float32)
    for k in range(col_count):
        for p in range(supers):
            piece = pieces[k][p][None, None]
            half_rows = lax.dynamic_update_slice(half_rows, piece, (p, col ^ k, 0, 0))
            ordered = lax.dynamic_update_slice(
                ordered, piece, (col ^ row ^ (p * cores), col ^ k, 0, 0)
            )
    for k in range(col_count):
        for p in range(supers):
            ordered = lax.dynamic_update_slice(
                ordered,
                pieces_core[k][p][None, None],
                (col ^ row ^ (p * cores + 1), col ^ k, 0, 0),
            )
    half_rows = half_rows.reshape(supers * block_rows, width)
    ordered = ordered.reshape(total_rows, width)
    sig_rows = jnp.concatenate(
        [jnp.concatenate([a, b], axis=0) for a, b in zip(sig, sig_partner)], axis=1
    )
    sig_rows, ordered = lax.optimization_barrier((sig_rows, ordered))

    scaled = jnp.dot(half_rows, dinv, precision=high)
    contract = (((0,), (0,)), ((), ()))
    d_half = lax.dynamic_slice_in_dim(dinv, core * half, half, 0)

    def band(value, index):
        return lax.dynamic_slice_in_dim(value, index * half, half, 1)

    gram = lax.dot_general(d_half, d_half, contract, precision=high)
    scaled_own = band(scaled, core)
    scaled_other = band(scaled, 1 - core)
    gram_own = unique_blocks(pick(gram.reshape(cores, half, width), core), core, tile)
    gram_other = unique_blocks(pick(gram.reshape(cores, half, width), 1 - core), 1 - core, tile)
    gram_own, gram_other, scaled_own, scaled_other = lax.optimization_barrier(
        (gram_own, gram_other, scaled_own, scaled_other)
    )
    weighted = jnp.dot(sig_rows, ordered, precision=high, preferred_element_type=jnp.float32)
    spread = jnp.dot(weighted, dinv, precision=high)

    spread_blocks = spread.reshape(supers, col_count, rows_dev, width)
    kept = pick(spread_blocks[0], col)
    got = other_plane(pick(spread_blocks[1], col))
    sel_off = pl.pallas_call(
        join_rows,
        out_shape=jax.ShapeDtypeStruct(anc_factor.shape, jnp.float32),
        cost_estimate=pl.CostEstimate(
            flops=0, transcendentals=0, bytes_accessed=8 * rows_dev * supers * width
        ),
        compiler_params=pltpu.CompilerParams(vmem_limit_bytes=8 * 4 * width * width),
        name="join_rows",
    )(own_mask, jnp.where(first, kept, got), jnp.where(first, got, kept))

    band_other = lax.dot_general(scaled_other, spread, contract, precision=high)
    sent = gram_other + unique_blocks(band_other, 1 - core, tile)
    received = other_core(sent)
    band_own = lax.dot_general(scaled_own, spread, contract, precision=high)
    finished = gram_own + unique_blocks(band_own, core, tile) + received
    far_finished = other_plane(finished)
    finished_core = other_core(finished)
    far_core = other_core(far_finished)
    square = place_square(supers, width, plane, core, [finished, finished_core])
    square = place_square(supers, width, 1 - plane, core, [far_finished], square)
    sel_diag = place_square(supers, width, 1 - plane, 1 - core, [far_core], square)
    return (sel_off, sel_diag)


def gather_fits(row_count, col_count, supers):
    return row_count == 2 * supers == 4 and col_count == 4


def body(sigma_anc, anc_factor, diag_inverse, pattern):
    supers = anc_factor.shape[1]
    if gather_fits(lax.axis_size("row"), lax.axis_size("col"), supers):
        return gather_body(sigma_anc, anc_factor, diag_inverse, pattern)
    return reduce_body(sigma_anc, anc_factor, diag_inverse, pattern)


def solution(mesh):
    return jax.shard_map(
        body,
        mesh=mesh,
        in_specs=(
            P(("grp", "row"), "col"),
            P(("grp", "row", "col"), None, None),
            P("grp", None, "row"),
            P(),
        ),
        out_specs=(P(("grp", "row", "col"), None, None), P("grp", None, None)),
        check_vma=False,
    )
```

```python
import functools

import jax
import jax.numpy as jnp
from jax import lax
from jax.experimental import pallas as pl
from jax.experimental.pallas import tpu as pltpu
from jax.sharding import PartitionSpec as P


def own_row_mask(pattern, rows_dev, position, total_rows):
    block_size = total_rows // pattern.shape[1]
    flat_mask = jnp.repeat(pattern.astype(jnp.float32), block_size, axis=1)
    return jnp.transpose(lax.dynamic_slice_in_dim(flat_mask, position * rows_dev, rows_dev, 1))[
        :, :, None
    ]


def reduce_body(sigma_anc, anc_factor, diag_inverse, pattern):
    precise = lax.Precision.HIGHEST
    rows_dev, _, super_width = anc_factor.shape
    row_count = lax.axis_size("row")
    col_count = lax.axis_size("col")
    position = lax.axis_index("row") * col_count + lax.axis_index("col")
    device_total = row_count * col_count
    own_mask = own_row_mask(pattern, rows_dev, position, rows_dev * device_total)
    share = -(-super_width // device_total)
    masked_factor = anc_factor * own_mask
    flattened = masked_factor.reshape(rows_dev, -1)
    gathered = lax.all_gather(flattened, "row", axis=0, tiled=True)
    stacked = gathered.reshape(row_count, rows_dev, flattened.shape[1])
    turned = lax.all_to_all(stacked, "col", split_axis=0, concat_axis=1, tiled=True)
    column_block = turned.reshape(row_count * rows_dev, flattened.shape[1])
    summed_rows = lax.psum_scatter(
        jnp.dot(sigma_anc, column_block, precision=precise, preferred_element_type=jnp.float32),
        "col",
        scatter_dimension=0,
        tiled=True,
    )
    off_factor = -(summed_rows.reshape(masked_factor.shape) * own_mask)
    both_rows = jnp.concatenate([masked_factor, off_factor], axis=0)
    column_piece = lax.all_gather(diag_inverse, "row", axis=2, tiled=True)
    product = jnp.einsum("rsk,skj->rsj", both_rows, column_piece, precision=precise)
    own_rows = lax.dynamic_slice_in_dim(column_piece, position * share, share, 1)
    scaled = product[:rows_dev]
    sel_off = product[rows_dev:]
    diag_term = jnp.einsum("skj,skl->sjl", own_rows, own_rows, precision=precise)
    partial_value = diag_term - jnp.einsum("rsj,rsl->sjl", scaled, sel_off, precision=precise)
    sel_diag = lax.psum(partial_value, ("row", "col"))
    return (sel_off, sel_diag)


def swap(value, axis, bit):
    count = lax.axis_size(axis)
    return lax.ppermute(value, axis, [(i, i ^ bit) for i in range(count)])


def unique_blocks(band, core, tile):
    base = core * 2 * tile
    blocks = []
    for i, j in ((0, 0), (0, 1), (1, 1)):
        blocks.append(lax.dynamic_slice(band, (i * tile, base + j * tile), (tile, tile)))
    for i in range(2):
        across = jnp.where(core == 0, 2 + i, 1 - i)
        blocks.append(lax.dynamic_slice(band, (i * tile, across * tile), (tile, tile)))
    return jnp.concatenate(blocks, axis=0)


def lay_out(tile, sources, place_ref, *refs):
    out_ref, turned, sems = refs[-3:]
    copies = []
    for step in range(sources):
        source = refs[step]
        core = lax.rem(place_ref[1] + step, 2)
        base = core * (2 * tile)

        def put(value, row, column):
            row, column = pl.multiple_of(row, tile), pl.multiple_of(column, tile)
            copies.append(
                pltpu.make_async_copy(
                    value,
                    out_ref.at[place_ref[0], pl.ds(row, tile), pl.ds(column, tile)],
                    sems.at[len(copies)],
                )
            )
            copies[-1].start()

        def block(i):
            return source.at[pl.ds(i * tile, tile), :]

        places = [(base, base + tile)]
        put(block(0), base, base)
        put(block(2), base + tile, base + tile)
        for i in range(2):
            places.append((base + i * tile, jnp.where(core == 0, 2 + i, 1 - i) * tile))
        for i, (block_id, (row, column)) in enumerate(zip((1, 3, 4), places)):
            put(block(block_id), row, column)
            turned[3 * step + i] = block(block_id)[...].T
            put(turned.at[3 * step + i], column, row)
    for copy in copies:
        copy.wait()


def place_square(supers, width, index, core, parts, target=None):
    tile = width // 4
    place = jnp.stack([index, core]).astype(jnp.int32)
    args = [place, *parts] + ([] if target is None else [target])
    return pl.pallas_call(
        functools.partial(lay_out, tile, len(parts)),
        out_shape=jax.ShapeDtypeStruct((supers, width, width), jnp.float32),
        in_specs=[pl.BlockSpec(memory_space=pltpu.SMEM)]
        + [pl.BlockSpec(memory_space=pltpu.VMEM)] * len(parts)
        + ([] if target is None else [pl.BlockSpec(memory_space=pl.ANY)]),
        out_specs=pl.BlockSpec(memory_space=pl.ANY),
        scratch_shapes=[
            pltpu.VMEM((3 * len(parts), tile, tile), jnp.float32),
            pltpu.SemaphoreType.DMA((8 * len(parts),)),
        ],
        input_output_aliases={} if target is None else {1 + len(parts): 0},
        cost_estimate=pl.CostEstimate(
            flops=0, transcendentals=0, bytes_accessed=2 * 4 * width * width
        ),
        compiler_params=pltpu.CompilerParams(vmem_limit_bytes=8 * 4 * width * width),
        name="lay_out_square",
    )(*args)


def join_rows(mask_ref, first_ref, second_ref, out_ref):
    out_ref[:, 0, :] = -(first_ref[...] * mask_ref[:, 0:1])
    out_ref[:, 1, :] = -(second_ref[...] * mask_ref[:, 1:2])


def gather_body(sigma_anc, anc_factor, diag_inverse, pattern):
    high = lax.Precision.HIGH
    rows_dev, supers, width = anc_factor.shape
    row_count = lax.axis_size("row")
    col_count = lax.axis_size("col")
    cores = row_count // supers
    row = lax.axis_index("row")
    col = lax.axis_index("col")
    plane = row // cores
    core = row % cores
    first = plane == 0
    block_rows = rows_dev * col_count
    total_rows = block_rows * row_count
    tile = width // 4
    half = width // cores

    def other_plane(value):
        return swap(value, "row", cores)

    def other_core(value):
        return swap(value, "row", 1)

    def pick(value, index):
        return lax.dynamic_index_in_dim(value, index, 0, keepdims=False)

    def along_col(value, partner):
        return swap(value, "col", partner)

    def at_super(value, index):
        return lax.dynamic_index_in_dim(value, index, 1, keepdims=False)

    theirs = at_super(anc_factor, 1 - plane)
    mine = at_super(anc_factor, plane)
    partner = other_plane(theirs)
    flat_mask = jnp.repeat(pattern.astype(jnp.float32), total_rows // pattern.shape[1], axis=1)

    def mask_at(block):
        return lax.dynamic_slice_in_dim(flat_mask, block * block_rows + col * rows_dev, rows_dev, 1)

    own_mask = jnp.transpose(mask_at(row))
    pair_mask = jnp.stack([pick(mask_at(row), plane), pick(mask_at(row ^ cores), plane)])
    masked = jnp.stack([mine, partner]) * pair_mask[:, :, None]
    pieces = [masked]
    pieces.append(along_col(masked, 1))
    pieces.append(along_col(masked, 2))
    pieces.append(along_col(pieces[2], 1))

    sig = [sigma_anc]
    for k in (1, 2, 3):
        sig.append(along_col(sigma_anc, k))
    sig_partner = [other_plane(sig[k]) for k in range(col_count)]

    share = diag_inverse.shape[2]
    d_own = pick(diag_inverse, plane)
    d_partner = other_plane(pick(diag_inverse, 1 - plane))
    d_pair = jnp.stack([d_own, d_partner])
    d_pair_core = other_core(d_pair)
    dinv = jnp.zeros((width, width), jnp.float32)
    for c, group in ((0, d_pair), (1, d_pair_core)):
        for p in range(supers):
            dinv = lax.dynamic_update_slice(dinv, group[p], (0, (row ^ (p * cores + c)) * share))

    scaled = []
    for k in range(col_count):
        flat = jnp.dot(pieces[k].reshape(supers * rows_dev, width), dinv, precision=high)
        scaled.append(flat.reshape(supers, rows_dev, width))
    scaled_core = [other_core(scaled[k]) for k in range(col_count)]
    last = col_count - 1
    half_rows = jnp.zeros((supers, col_count, rows_dev, width), jnp.float32)
    early = jnp.zeros((row_count, col_count, rows_dev, width), jnp.float32)
    late = jnp.zeros((row_count, rows_dev, width), jnp.float32)
    for k in range(col_count):
        for p in range(supers):
            half_rows = lax.dynamic_update_slice(
                half_rows, scaled[k][p][None, None], (p, col ^ k, 0, 0)
            )
            for c, group in ((0, scaled[k]), (1, scaled_core[k])):
                block = col ^ row ^ (p * cores + c)
                if k < last:
                    early = lax.dynamic_update_slice(
                        early, group[p][None, None], (block, col ^ k, 0, 0)
                    )
                else:
                    late = lax.dynamic_update_slice(late, group[p][None], (block, 0, 0))
    half_rows = half_rows.reshape(supers * block_rows, width)
    early = early.reshape(total_rows, width)
    late = late.reshape(row_count * rows_dev, width)
    sig_pairs = [jnp.concatenate([a, b], axis=0) for a, b in zip(sig, sig_partner)]
    sig_rows = jnp.concatenate(sig_pairs, axis=1)
    sig_late = jnp.concatenate(
        [lax.dynamic_slice_in_dim(v, (col ^ last) * rows_dev, rows_dev, 1) for v in sig_pairs],
        axis=1,
    )
    sig_rows, sig_late, early = lax.optimization_barrier((sig_rows, sig_late, early))
    spread_early = jnp.dot(
        sig_rows, early, precision=high, preferred_element_type=jnp.float32
    )
    spread_early, late = lax.optimization_barrier((spread_early, late))
    spread = spread_early + jnp.dot(
        sig_late, late, precision=high, preferred_element_type=jnp.float32
    )

    contract = (((0,), (0,)), ((), ()))
    d_half = lax.dynamic_slice_in_dim(dinv, core * half, half, 0)

    def band(value, index):
        return lax.dynamic_slice_in_dim(value, index * half, half, 1)

    gram = lax.dot_general(d_half, d_half, contract, precision=high)
    gram_own = unique_blocks(pick(gram.reshape(cores, half, width), core), core, tile)
    gram_other = unique_blocks(pick(gram.reshape(cores, half, width), 1 - core), 1 - core, tile)
    gram_own, gram_other = lax.optimization_barrier((gram_own, gram_other))
    scaled_own = band(half_rows, core)
    scaled_other = band(half_rows, 1 - core)
    scaled_own, scaled_other = lax.optimization_barrier((scaled_own, scaled_other))

    spread_blocks = spread.reshape(supers, col_count, rows_dev, width)
    kept = pick(spread_blocks[0], col)
    got = other_plane(pick(spread_blocks[1], col))
    sel_off = pl.pallas_call(
        join_rows,
        out_shape=jax.ShapeDtypeStruct(anc_factor.shape, jnp.float32),
        cost_estimate=pl.CostEstimate(
            flops=0, transcendentals=0, bytes_accessed=8 * rows_dev * supers * width
        ),
        compiler_params=pltpu.CompilerParams(vmem_limit_bytes=8 * 4 * width * width),
        name="join_rows",
    )(own_mask, jnp.where(first, kept, got), jnp.where(first, got, kept))

    band_other = lax.dot_general(scaled_other, spread, contract, precision=high)
    sent = gram_other + unique_blocks(band_other, 1 - core, tile)
    received = other_core(sent)
    band_own = lax.dot_general(scaled_own, spread, contract, precision=high)
    finished = gram_own + unique_blocks(band_own, core, tile) + received
    far_finished = other_plane(finished)
    finished_core = other_core(finished)
    far_core = other_core(far_finished)
    square = place_square(supers, width, plane, core, [finished, finished_core])
    square = place_square(supers, width, 1 - plane, core, [far_finished], square)
    sel_diag = place_square(supers, width, 1 - plane, 1 - core, [far_core], square)
    return (sel_off, sel_diag)


def gather_fits(row_count, col_count, supers):
    return row_count == 2 * supers == 4 and col_count == 4


def body(sigma_anc, anc_factor, diag_inverse, pattern):
    supers = anc_factor.shape[1]
    if gather_fits(lax.axis_size("row"), lax.axis_size("col"), supers):
        return gather_body(sigma_anc, anc_factor, diag_inverse, pattern)
    return reduce_body(sigma_anc, anc_factor, diag_inverse, pattern)


def solution(mesh):
    return jax.shard_map(
        body,
        mesh=mesh,
        in_specs=(
            P(("grp", "row"), "col"),
            P(("grp", "row", "col"), None, None),
            P("grp", None, "row"),
            P(),
        ),
        out_specs=(P(("grp", "row", "col"), None, None), P("grp", None, None)),
        check_vma=False,
    )
```

```python
import functools

import jax
import jax.numpy as jnp
from jax import lax
from jax.experimental import pallas as pl
from jax.experimental.pallas import tpu as pltpu
from jax.sharding import PartitionSpec as P


def own_row_mask(pattern, rows_dev, position, total_rows):
    block_size = total_rows // pattern.shape[1]
    flat_mask = jnp.repeat(pattern.astype(jnp.float32), block_size, axis=1)
    return jnp.transpose(lax.dynamic_slice_in_dim(flat_mask, position * rows_dev, rows_dev, 1))[
        :, :, None
    ]


def reduce_body(sigma_anc, anc_factor, diag_inverse, pattern):
    precise = lax.Precision.HIGHEST
    rows_dev, _, super_width = anc_factor.shape
    row_count = lax.axis_size("row")
    col_count = lax.axis_size("col")
    position = lax.axis_index("row") * col_count + lax.axis_index("col")
    device_total = row_count * col_count
    own_mask = own_row_mask(pattern, rows_dev, position, rows_dev * device_total)
    share = -(-super_width // device_total)
    masked_factor = anc_factor * own_mask
    flattened = masked_factor.reshape(rows_dev, -1)
    gathered = lax.all_gather(flattened, "row", axis=0, tiled=True)
    stacked = gathered.reshape(row_count, rows_dev, flattened.shape[1])
    turned = lax.all_to_all(stacked, "col", split_axis=0, concat_axis=1, tiled=True)
    column_block = turned.reshape(row_count * rows_dev, flattened.shape[1])
    summed_rows = lax.psum_scatter(
        jnp.dot(sigma_anc, column_block, precision=precise, preferred_element_type=jnp.float32),
        "col",
        scatter_dimension=0,
        tiled=True,
    )
    off_factor = -(summed_rows.reshape(masked_factor.shape) * own_mask)
    both_rows = jnp.concatenate([masked_factor, off_factor], axis=0)
    column_piece = lax.all_gather(diag_inverse, "row", axis=2, tiled=True)
    product = jnp.einsum("rsk,skj->rsj", both_rows, column_piece, precision=precise)
    own_rows = lax.dynamic_slice_in_dim(column_piece, position * share, share, 1)
    scaled = product[:rows_dev]
    sel_off = product[rows_dev:]
    diag_term = jnp.einsum("skj,skl->sjl", own_rows, own_rows, precision=precise)
    partial_value = diag_term - jnp.einsum("rsj,rsl->sjl", scaled, sel_off, precision=precise)
    sel_diag = lax.psum(partial_value, ("row", "col"))
    return (sel_off, sel_diag)


def swap(value, axis, bit):
    count = lax.axis_size(axis)
    return lax.ppermute(value, axis, [(i, i ^ bit) for i in range(count)])


def unique_blocks(band, core, tile):
    base = core * 2 * tile
    blocks = []
    for i, j in ((0, 0), (0, 1), (1, 1)):
        blocks.append(lax.dynamic_slice(band, (i * tile, base + j * tile), (tile, tile)))
    for i in range(2):
        across = jnp.where(core == 0, 2 + i, 1 - i)
        blocks.append(lax.dynamic_slice(band, (i * tile, across * tile), (tile, tile)))
    return jnp.concatenate(blocks, axis=0)


def lay_out(tile, sources, place_ref, *refs):
    out_ref, turned, sems = refs[-3:]
    copies = []
    for step in range(sources):
        source = refs[step]
        core = lax.rem(place_ref[1] + step, 2)
        base = core * (2 * tile)

        def put(value, row, column):
            row, column = pl.multiple_of(row, tile), pl.multiple_of(column, tile)
            copies.append(
                pltpu.make_async_copy(
                    value,
                    out_ref.at[place_ref[0], pl.ds(row, tile), pl.ds(column, tile)],
                    sems.at[len(copies)],
                )
            )
            copies[-1].start()

        def block(i):
            return source.at[pl.ds(i * tile, tile), :]

        places = [(base, base + tile)]
        put(block(0), base, base)
        put(block(2), base + tile, base + tile)
        for i in range(2):
            places.append((base + i * tile, jnp.where(core == 0, 2 + i, 1 - i) * tile))
        for i, (block_id, (row, column)) in enumerate(zip((1, 3, 4), places)):
            put(block(block_id), row, column)
            turned[3 * step + i] = block(block_id)[...].T
            put(turned.at[3 * step + i], column, row)
    for copy in copies:
        copy.wait()


def place_square(supers, width, index, core, parts, target=None):
    tile = width // 4
    place = jnp.stack([index, core]).astype(jnp.int32)
    args = [place, *parts] + ([] if target is None else [target])
    return pl.pallas_call(
        functools.partial(lay_out, tile, len(parts)),
        out_shape=jax.ShapeDtypeStruct((supers, width, width), jnp.float32),
        in_specs=[pl.BlockSpec(memory_space=pltpu.SMEM)]
        + [pl.BlockSpec(memory_space=pltpu.VMEM)] * len(parts)
        + ([] if target is None else [pl.BlockSpec(memory_space=pl.ANY)]),
        out_specs=pl.BlockSpec(memory_space=pl.ANY),
        scratch_shapes=[
            pltpu.VMEM((3 * len(parts), tile, tile), jnp.float32),
            pltpu.SemaphoreType.DMA((8 * len(parts),)),
        ],
        input_output_aliases={} if target is None else {1 + len(parts): 0},
        cost_estimate=pl.CostEstimate(
            flops=0, transcendentals=0, bytes_accessed=2 * 4 * width * width
        ),
        compiler_params=pltpu.CompilerParams(vmem_limit_bytes=8 * 4 * width * width),
        name="lay_out_square",
    )(*args)


def join_rows(mask_ref, first_ref, second_ref, out_ref):
    out_ref[:, 0, :] = -(first_ref[...] * mask_ref[:, 0:1])
    out_ref[:, 1, :] = -(second_ref[...] * mask_ref[:, 1:2])


def gather_body(sigma_anc, anc_factor, diag_inverse, pattern):
    high = lax.Precision.HIGH
    rows_dev, supers, width = anc_factor.shape
    row_count = lax.axis_size("row")
    col_count = lax.axis_size("col")
    cores = row_count // supers
    row = lax.axis_index("row")
    col = lax.axis_index("col")
    plane = row // cores
    core = row % cores
    first = plane == 0
    block_rows = rows_dev * col_count
    total_rows = block_rows * row_count
    tile = width // 4
    half = width // cores

    def other_plane(value):
        return swap(value, "row", cores)

    def other_core(value):
        return swap(value, "row", 1)

    def pick(value, index):
        return lax.dynamic_index_in_dim(value, index, 0, keepdims=False)

    def along_col(value, partner):
        return swap(value, "col", partner)

    def at_super(value, index):
        return lax.dynamic_index_in_dim(value, index, 1, keepdims=False)

    mine = at_super(anc_factor, plane)
    partner = other_plane(at_super(anc_factor, 1 - plane))
    rows_sent = jnp.stack([mine, partner])
    far = along_col(rows_sent, 2)
    near = along_col(rows_sent, 1)
    pieces = [rows_sent, near, far, along_col(far, 1)]
    flat_mask = jnp.repeat(pattern.astype(jnp.float32), total_rows // pattern.shape[1], axis=1)
    own_mask = jnp.transpose(
        lax.dynamic_slice_in_dim(flat_mask, row * block_rows + col * rows_dev, rows_dev, 1)
    )
    super_mask = pick(flat_mask, plane)

    def piece_mask(p, k):
        start = (row ^ (p * cores)) * block_rows + (col ^ k) * rows_dev
        return lax.dynamic_slice_in_dim(super_mask, start, rows_dev, 0)

    sig = [sigma_anc, along_col(sigma_anc, 1), along_col(sigma_anc, 2)]
    sig.append(along_col(sig[2], 1))
    sig_partner = [other_plane(sig[k]) for k in range(col_count)]

    share = diag_inverse.shape[2]
    d_own = pick(diag_inverse, plane)
    d_partner = other_plane(pick(diag_inverse, 1 - plane))
    d_pair = jnp.stack([d_own, d_partner])
    d_pair_core = other_core(d_pair)
    dinv = jnp.zeros((width, width), jnp.float32)
    for c, group in ((0, d_pair), (1, d_pair_core)):
        for p in range(supers):
            dinv = lax.dynamic_update_slice(dinv, group[p], (0, (row ^ (p * cores + c)) * share))

    rows = jnp.concatenate(pieces, axis=0).reshape(supers * block_rows, width)
    row_masks = [piece_mask(p, k) for k in range(col_count) for p in range(supers)]
    row_mask = lax.optimization_barrier(jnp.concatenate(row_masks, axis=0))
    scaled = jnp.dot(rows, dinv, precision=high) * row_mask[:, None]
    scaled = scaled.reshape(col_count, supers, rows_dev, width)
    scaled_core = other_core(scaled)
    half_rows = jnp.zeros((supers, col_count, rows_dev, width), jnp.float32)
    ordered = jnp.zeros((row_count, col_count, rows_dev, width), jnp.float32)
    for k in range(col_count):
        for p in range(supers):
            half_rows = lax.dynamic_update_slice(
                half_rows, scaled[k, p][None, None], (p, col ^ k, 0, 0)
            )
            for c, group in ((0, scaled), (1, scaled_core)):
                block = col ^ row ^ (p * cores + c)
                ordered = lax.dynamic_update_slice(
                    ordered, group[k, p][None, None], (block, col ^ k, 0, 0)
                )
    half_rows = half_rows.reshape(supers * block_rows, width)
    ordered = ordered.reshape(total_rows, width)
    (sig, sig_partner), scaled = lax.optimization_barrier(((sig, sig_partner), scaled))
    sig_pairs = [jnp.concatenate([a, b], axis=0) for a, b in zip(sig, sig_partner)]
    sig_rows = jnp.concatenate(sig_pairs, axis=1)
    sig_rows, ordered = lax.optimization_barrier((sig_rows, ordered))
    spread = jnp.dot(sig_rows, ordered, precision=high, preferred_element_type=jnp.float32)

    contract = (((0,), (0,)), ((), ()))
    d_half = lax.dynamic_slice_in_dim(dinv, core * half, half, 0)

    def band(value, index):
        return lax.dynamic_slice_in_dim(value, index * half, half, 1)

    gram = lax.dot_general(d_half, d_half, contract, precision=high)
    gram_own = unique_blocks(pick(gram.reshape(cores, half, width), core), core, tile)
    gram_other = unique_blocks(pick(gram.reshape(cores, half, width), 1 - core), 1 - core, tile)
    gram_own, gram_other = lax.optimization_barrier((gram_own, gram_other))
    scaled_own = band(half_rows, core)
    scaled_other = band(half_rows, 1 - core)
    scaled_own, scaled_other = lax.optimization_barrier((scaled_own, scaled_other))

    spread_blocks = spread.reshape(supers, col_count, rows_dev, width)
    kept = pick(spread_blocks[0], col)
    got = other_plane(pick(spread_blocks[1], col))
    sel_off = pl.pallas_call(
        join_rows,
        out_shape=jax.ShapeDtypeStruct(anc_factor.shape, jnp.float32),
        cost_estimate=pl.CostEstimate(
            flops=0, transcendentals=0, bytes_accessed=8 * rows_dev * supers * width
        ),
        compiler_params=pltpu.CompilerParams(vmem_limit_bytes=8 * 4 * width * width),
        name="join_rows",
    )(own_mask, jnp.where(first, kept, got), jnp.where(first, got, kept))

    band_other = lax.dot_general(scaled_other, spread, contract, precision=high)
    sent = gram_other + unique_blocks(band_other, 1 - core, tile)
    received = other_core(sent)
    band_own = lax.dot_general(scaled_own, spread, contract, precision=high)
    finished = gram_own + unique_blocks(band_own, core, tile) + received
    far_finished = other_plane(finished)
    finished_core = other_core(finished)
    far_core = other_core(far_finished)
    square = place_square(supers, width, plane, core, [finished, finished_core])
    square = place_square(supers, width, 1 - plane, core, [far_finished], square)
    sel_diag = place_square(supers, width, 1 - plane, 1 - core, [far_core], square)
    return (sel_off, sel_diag)


def gather_fits(row_count, col_count, supers):
    return row_count == 2 * supers == 4 and col_count == 4


def body(sigma_anc, anc_factor, diag_inverse, pattern):
    supers = anc_factor.shape[1]
    if gather_fits(lax.axis_size("row"), lax.axis_size("col"), supers):
        return gather_body(sigma_anc, anc_factor, diag_inverse, pattern)
    return reduce_body(sigma_anc, anc_factor, diag_inverse, pattern)


def solution(mesh):
    return jax.shard_map(
        body,
        mesh=mesh,
        in_specs=(
            P(("grp", "row"), "col"),
            P(("grp", "row", "col"), None, None),
            P("grp", None, "row"),
            P(),
        ),
        out_specs=(P(("grp", "row", "col"), None, None), P("grp", None, None)),
        check_vma=False,
    )
```

```python
import functools

import jax
import jax.numpy as jnp
from jax import lax
from jax.experimental import pallas as pl
from jax.experimental.pallas import tpu as pltpu
from jax.sharding import PartitionSpec as P


def own_row_mask(pattern, rows_dev, position, total_rows):
    block_size = total_rows // pattern.shape[1]
    flat_mask = jnp.repeat(pattern.astype(jnp.float32), block_size, axis=1)
    return jnp.transpose(lax.dynamic_slice_in_dim(flat_mask, position * rows_dev, rows_dev, 1))[
        :, :, None
    ]


def reduce_body(sigma_anc, anc_factor, diag_inverse, pattern):
    precise = lax.Precision.HIGHEST
    rows_dev, _, super_width = anc_factor.shape
    row_count = lax.axis_size("row")
    col_count = lax.axis_size("col")
    position = lax.axis_index("row") * col_count + lax.axis_index("col")
    device_total = row_count * col_count
    own_mask = own_row_mask(pattern, rows_dev, position, rows_dev * device_total)
    share = -(-super_width // device_total)
    masked_factor = anc_factor * own_mask
    flattened = masked_factor.reshape(rows_dev, -1)
    gathered = lax.all_gather(flattened, "row", axis=0, tiled=True)
    stacked = gathered.reshape(row_count, rows_dev, flattened.shape[1])
    turned = lax.all_to_all(stacked, "col", split_axis=0, concat_axis=1, tiled=True)
    column_block = turned.reshape(row_count * rows_dev, flattened.shape[1])
    summed_rows = lax.psum_scatter(
        jnp.dot(sigma_anc, column_block, precision=precise, preferred_element_type=jnp.float32),
        "col",
        scatter_dimension=0,
        tiled=True,
    )
    off_factor = -(summed_rows.reshape(masked_factor.shape) * own_mask)
    both_rows = jnp.concatenate([masked_factor, off_factor], axis=0)
    column_piece = lax.all_gather(diag_inverse, "row", axis=2, tiled=True)
    product = jnp.einsum("rsk,skj->rsj", both_rows, column_piece, precision=precise)
    own_rows = lax.dynamic_slice_in_dim(column_piece, position * share, share, 1)
    scaled = product[:rows_dev]
    sel_off = product[rows_dev:]
    diag_term = jnp.einsum("skj,skl->sjl", own_rows, own_rows, precision=precise)
    partial_value = diag_term - jnp.einsum("rsj,rsl->sjl", scaled, sel_off, precision=precise)
    sel_diag = lax.psum(partial_value, ("row", "col"))
    return (sel_off, sel_diag)


def swap(value, axis, bit):
    count = lax.axis_size(axis)
    return lax.ppermute(value, axis, [(i, i ^ bit) for i in range(count)])


def halves(value):
    high = value.astype(jnp.bfloat16)
    return high, (value - high.astype(jnp.float32)).astype(jnp.bfloat16)


ROWS_BY_COLUMNS = (((1,), (0,)), ((), ()))


def product3(left, right, dims):
    def one(a, b):
        return lax.dot_general(a, b, dims, preferred_element_type=jnp.float32)

    return one(left[0], right[0]) + (one(left[0], right[1]) + one(left[1], right[0]))


def unique_tiles(core, tile):
    base = core * (2 * tile)
    tiles = [(base, base), (base, base + tile), (base + tile, base + tile)]
    for i in range(2):
        tiles.append((base + i * tile, jnp.where(core == 0, 2 + i, 1 - i) * tile))
    return [(pl.multiple_of(i, tile), pl.multiple_of(j, tile)) for i, j in tiles]


def put_unique(out, extra, band, core, tile):
    base = core * (2 * tile)
    for n, (i, j) in enumerate(unique_tiles(core, tile)):
        at = pl.ds(n * tile, tile)
        value = band[pl.ds(pl.multiple_of(i - base, tile), tile), pl.ds(j, tile)]
        out[at, :] = value if extra is None else value + extra[at, :]


def inverse_kernel(cores, own, partner, own_core, partner_core, *refs):
    high, low, gram_own, gram_other, band = refs
    row = lax.axis_index("row")
    share = own.shape[1]
    width = high.shape[0]
    tile = width // 4
    for step, value in enumerate((own, own_core, partner, partner_core)):
        place = pl.ds(pl.multiple_of((row ^ step) * share, share), share)
        high[:, place], low[:, place] = halves(value[...])
    core = lax.rem(row, cores)
    half = width // cores
    rows = pl.ds(pl.multiple_of(core * half, half), half)
    for who, out in ((core, gram_own), (1 - core, gram_other)):
        columns = pl.ds(pl.multiple_of(who * half, half), half)
        left = (high[rows, columns].T, low[rows, columns].T)
        band[...] = product3(left, (high[rows, :], low[rows, :]), ROWS_BY_COLUMNS)
        put_unique(out, None, band, who, tile)


def scale_kernel(ks, cores, cols, block_size, pattern_ref, high, low, *refs):
    pieces, out, split_high, split_low = refs[:-3], refs[-3], refs[-2], refs[-1]
    row, col = lax.axis_index("row"), lax.axis_index("col")
    supers, rows_dev, _ = pieces[0].shape
    for n, piece in enumerate(pieces):
        for p in range(supers):
            at = pl.ds((n * supers + p) * rows_dev, rows_dev)
            split_high[at, :], split_low[at, :] = halves(piece[p])
    scaled = product3(
        (split_high[...], split_low[...]), (high[...], low[...]), ROWS_BY_COLUMNS
    )
    present = pattern_ref[pl.ds(row // cores, 1), :].astype(jnp.float32)
    index = lax.broadcasted_iota(jnp.int32, (rows_dev, 1), 0)
    for n, k in enumerate(ks):
        for p in range(supers):
            start = ((row ^ (p * cores)) * cols + (col ^ k)) * rows_dev
            mask = jnp.zeros((rows_dev, 1), jnp.float32)
            for b in range(pattern_ref.shape[1]):
                inside = (index + start >= b * block_size) & (index + start < (b + 1) * block_size)
                mask = jnp.where(inside, present[:, b : b + 1], mask)
            first = (n * supers + p) * rows_dev
            out[n, p] = scaled[first : first + rows_dev] * mask


def prepare_kernel(cols, pad, ks, *refs):
    sig = refs[:cols]
    partner = refs[cols : 2 * cols]
    groups = refs[2 * cols : 2 * cols + 2]
    left_high, left_low, turned_high, turned_low, rows_high, rows_low = refs[2 * cols + 2 :]
    col = lax.axis_index("col")
    _, supers, rows_dev, _ = groups[0].shape
    block = sig[0].shape[0]
    for k in range(cols):
        for n, source in enumerate((sig[k], partner[k])):
            at = pl.ds(n * block, block)
            for ref, value in zip((left_high, left_low), halves(source[...])):
                ref[at, pl.ds(k * pad, block)] = value
                ref[at, pl.ds(k * pad + block, pad - block)] = jnp.zeros(
                    (block, pad - block), ref.dtype
                )
    for group, members in zip(groups, ks):
        for n, k in enumerate(members):
            for p in range(supers):
                at = pl.ds(pl.multiple_of(p * block + (col ^ k) * rows_dev, 16), rows_dev)
                rows_high[at, :], rows_low[at, :] = halves(group[n, p])
    turned_high[...] = rows_high[...].T
    turned_low[...] = rows_low[...].T


def product_kernel(cores, cols, pad, ks, gram_other, *refs):
    left_high, left_low, turned_high, turned_low = refs[:4]
    groups, groups_core = refs[4:6], refs[6:8]
    sent, kept, away, y_high, y_low, right_high, right_low, band = refs[8:]
    row, col = lax.axis_index("row"), lax.axis_index("col")
    _, supers, rows_dev, width = groups[0].shape
    block = y_high.shape[0] // supers
    tile = width // 4
    half = width // cores
    for ref in (right_high, right_low):
        for k in range(cols):
            ref[pl.ds(k * pad + block, pad - block), :] = jnp.zeros((pad - block, width), ref.dtype)
    for c, source in enumerate((groups, groups_core)):
        for group, members in zip(source, ks):
            for n, k in enumerate(members):
                for p in range(supers):
                    which = (col ^ row) ^ (p * cores + c)
                    at = pl.multiple_of(which * pad + (col ^ k) * rows_dev, 16)
                    at = pl.ds(at, rows_dev)
                    right_high[at, :], right_low[at, :] = halves(group[n, p])
    spread = product3(
        (left_high[...], left_low[...]), (right_high[...], right_low[...]), ROWS_BY_COLUMNS
    )
    y_high[...], y_low[...] = halves(spread)

    def rows_at(start):
        at = pl.ds(pl.multiple_of(start + col * rows_dev, 16), rows_dev)
        return y_high[at, :].astype(jnp.float32) + y_low[at, :].astype(jnp.float32)

    kept[...] = rows_at(0)
    sent[...] = rows_at(block)
    other = 1 - lax.rem(row, cores)
    at = pl.ds(pl.multiple_of(other * half, half), half)
    left = (turned_high[at, :], turned_low[at, :])
    band[...] = product3(left, (y_high[...], y_low[...]), ROWS_BY_COLUMNS)
    put_unique(away, gram_other, band, other, tile)


def own_kernel(cores, gram_own, turned_high, turned_low, y_high, y_low, out, band):
    core = lax.rem(lax.axis_index("row"), cores)
    half = band.shape[0]
    at = pl.ds(pl.multiple_of(core * half, half), half)
    left = (turned_high[at, :], turned_low[at, :])
    band[...] = product3(left, (y_high[...], y_low[...]), ROWS_BY_COLUMNS)
    put_unique(out, gram_own, band, core, out.shape[1])


def local_call(kernel, outs, scratch, args, flops, limit):
    in_specs = [pl.BlockSpec(memory_space=pltpu.VMEM)] * len(args)
    moved = sum(a.size * a.dtype.itemsize for a in list(args) + list(outs))
    return pl.pallas_call(
        kernel,
        out_shape=outs,
        in_specs=in_specs,
        out_specs=[pl.BlockSpec(memory_space=pltpu.VMEM)] * len(outs),
        scratch_shapes=scratch,
        cost_estimate=pl.CostEstimate(flops=flops, transcendentals=0, bytes_accessed=moved),
        compiler_params=pltpu.CompilerParams(vmem_limit_bytes=limit),
    )(*args)


def lay_out(tile, sources, cores, away, flip, *refs):
    out_ref, turned, sems = refs[-3:]
    row = lax.axis_index("row")
    index = (row // cores) ^ away
    copies = []

    def put(value, i, j):
        i, j = pl.multiple_of(i, tile), pl.multiple_of(j, tile)
        target = out_ref.at[index, pl.ds(i, tile), pl.ds(j, tile)]
        copies.append(pltpu.make_async_copy(value, target, sems.at[len(copies)]))
        copies[-1].start()

    mirrored = []
    for step in range(sources):
        source = refs[step]
        tiles = unique_tiles(lax.rem(row, cores) ^ step ^ flip, tile)
        for n, (i, j) in enumerate(tiles):
            at = pl.ds(n * tile, tile)
            put(source.at[at, :], i, j)
            if n not in (0, 2):
                turned[len(mirrored)] = source[at, :].T
                mirrored.append((j, i))
    for n, (i, j) in enumerate(mirrored):
        put(turned.at[n], i, j)
    for copy in copies:
        copy.wait()


def place_square(supers, width, cores, away, flip, parts, target=None):
    tile = width // 4
    args = [*parts] + ([] if target is None else [target])
    return pl.pallas_call(
        functools.partial(lay_out, tile, len(parts), cores, away, flip),
        out_shape=jax.ShapeDtypeStruct((supers, width, width), jnp.float32),
        in_specs=[pl.BlockSpec(memory_space=pltpu.VMEM)] * len(parts)
        + ([] if target is None else [pl.BlockSpec(memory_space=pl.ANY)]),
        out_specs=pl.BlockSpec(memory_space=pl.ANY),
        scratch_shapes=[
            pltpu.VMEM((3 * len(parts), tile, tile), jnp.float32),
            pltpu.SemaphoreType.DMA((8 * len(parts),)),
        ],
        input_output_aliases={} if target is None else {len(parts): 0},
        cost_estimate=pl.CostEstimate(
            flops=0, transcendentals=0, bytes_accessed=2 * 4 * width * width
        ),
        compiler_params=pltpu.CompilerParams(vmem_limit_bytes=8 * 4 * width * width),
        name="lay_out_square",
    )(*args)


def join_rows(mask_ref, first_ref, second_ref, out_ref):
    out_ref[:, 0, :] = -(first_ref[...] * mask_ref[:, 0:1])
    out_ref[:, 1, :] = -(second_ref[...] * mask_ref[:, 1:2])


def gather_body(sigma_anc, anc_factor, diag_inverse, pattern):
    high = lax.Precision.HIGH
    rows_dev, supers, width = anc_factor.shape
    row_count = lax.axis_size("row")
    col_count = lax.axis_size("col")
    cores = row_count // supers
    row = lax.axis_index("row")
    col = lax.axis_index("col")
    plane = row // cores
    first = plane == 0
    block_rows = rows_dev * col_count
    total_rows = block_rows * row_count
    tile = width // 4
    half = width // cores

    def other_plane(value):
        return swap(value, "row", cores)

    def other_core(value):
        return swap(value, "row", 1)

    def pick(value, index):
        return lax.dynamic_index_in_dim(value, index, 0, keepdims=False)

    def along_col(value, partner):
        return swap(value, "col", partner)

    def at_super(value, index):
        return lax.dynamic_index_in_dim(value, index, 1, keepdims=False)

    mine = at_super(anc_factor, plane)
    partner = other_plane(at_super(anc_factor, 1 - plane))
    rows_sent = jnp.stack([mine, partner])
    far = along_col(rows_sent, 2)
    near = along_col(rows_sent, 1)
    pieces = [rows_sent, near, far, along_col(far, 1)]
    flat_mask = jnp.repeat(pattern.astype(jnp.float32), total_rows // pattern.shape[1], axis=1)
    own_mask = jnp.transpose(
        lax.dynamic_slice_in_dim(flat_mask, row * block_rows + col * rows_dev, rows_dev, 1)
    )

    sig = [sigma_anc, along_col(sigma_anc, 1), along_col(sigma_anc, 2)]
    sig.append(along_col(sig[2], 1))
    sig_partner = [other_plane(sig[k]) for k in range(col_count)]

    d_own = pick(diag_inverse, plane)
    d_partner = other_plane(pick(diag_inverse, 1 - plane))
    d_own_core = other_core(d_own)
    d_partner_core = other_core(d_partner)

    def shaped(shape, dtype=jnp.float32):
        return jax.ShapeDtypeStruct(shape, dtype)

    wide = shaped((width, width), jnp.bfloat16)
    unique = shaped((5 * tile, tile))
    square_bytes = 4 * width * width
    band = pltpu.VMEM((half, width), jnp.float32)
    high, low, gram_own, gram_other = local_call(
        functools.partial(inverse_kernel, cores),
        [wide, wide, unique, unique],
        [band],
        [d_own, d_partner, d_own_core, d_partner_core],
        6 * half * half * width,
        8 * square_bytes,
    )

    ks = ((0, 2), (1, 3))

    def scale(members):
        count = len(members) * supers * rows_dev
        return local_call(
            functools.partial(
                scale_kernel, members, cores, col_count, total_rows // pattern.shape[1]
            ),
            [shaped((len(members), supers, rows_dev, width))],
            [pltpu.VMEM((count, width), jnp.bfloat16)] * 2,
            [pattern, high, low] + [pieces[k] for k in members],
            6 * count * width * width,
            8 * square_bytes,
        )[0]

    early = scale(ks[0])
    early_core = other_core(early)
    late = scale(ks[1])
    late_core = other_core(late)
    pad = -(-block_rows // 256) * 256
    x_rows = supers * block_rows
    left_high, left_low, turned_high, turned_low = local_call(
        functools.partial(prepare_kernel, col_count, pad, ks),
        [shaped((x_rows, col_count * pad), jnp.bfloat16)] * 2
        + [shaped((width, x_rows), jnp.bfloat16)] * 2,
        [pltpu.VMEM((x_rows, width), jnp.bfloat16)] * 2,
        [*sig, *sig_partner, early, late],
        x_rows * total_rows,
        8 * square_bytes,
    )
    split = shaped((x_rows, width), jnp.bfloat16)
    rows_out = shaped((rows_dev, width))
    sent, kept, away, y_high, y_low = local_call(
        functools.partial(product_kernel, cores, col_count, pad, ks),
        [rows_out, rows_out, unique, split, split],
        [pltpu.VMEM((col_count * pad, width), jnp.bfloat16)] * 2 + [band],
        [gram_other, left_high, left_low, turned_high, turned_low]
        + [early, late, early_core, late_core],
        6 * x_rows * total_rows * width,
        16 * square_bytes,
    )

    got = other_plane(sent)
    sel_off = pl.pallas_call(
        join_rows,
        out_shape=jax.ShapeDtypeStruct(anc_factor.shape, jnp.float32),
        cost_estimate=pl.CostEstimate(
            flops=0, transcendentals=0, bytes_accessed=8 * rows_dev * supers * width
        ),
        compiler_params=pltpu.CompilerParams(vmem_limit_bytes=8 * 4 * width * width),
        name="join_rows",
    )(own_mask, jnp.where(first, kept, got), jnp.where(first, got, kept))

    received = other_core(away)
    (own_blocks,) = local_call(
        functools.partial(own_kernel, cores),
        [unique],
        [band],
        [gram_own, turned_high, turned_low, y_high, y_low],
        6 * half * x_rows * width,
        8 * square_bytes,
    )
    finished = own_blocks + received
    far_finished = other_plane(finished)
    finished_core = other_core(finished)
    far_core = other_core(far_finished)
    square = place_square(supers, width, cores, 0, 0, [finished, finished_core])
    square = place_square(supers, width, cores, 1, 0, [far_finished], square)
    sel_diag = place_square(supers, width, cores, 1, 1, [far_core], square)
    return (sel_off, sel_diag)


def gather_fits(row_count, col_count, supers):
    return row_count == 2 * supers == 4 and col_count == 4


def body(sigma_anc, anc_factor, diag_inverse, pattern):
    supers = anc_factor.shape[1]
    if gather_fits(lax.axis_size("row"), lax.axis_size("col"), supers):
        return gather_body(sigma_anc, anc_factor, diag_inverse, pattern)
    return reduce_body(sigma_anc, anc_factor, diag_inverse, pattern)


def solution(mesh):
    return jax.shard_map(
        body,
        mesh=mesh,
        in_specs=(
            P(("grp", "row"), "col"),
            P(("grp", "row", "col"), None, None),
            P("grp", None, "row"),
            P(),
        ),
        out_specs=(P(("grp", "row", "col"), None, None), P("grp", None, None)),
        check_vma=False,
    )
```

```python
import functools

import jax
import jax.numpy as jnp
from jax import lax
from jax.experimental import pallas as pl
from jax.experimental.pallas import tpu as pltpu
from jax.sharding import PartitionSpec as P


def own_row_mask(pattern, rows_dev, position, total_rows):
    block_size = total_rows // pattern.shape[1]
    flat_mask = jnp.repeat(pattern.astype(jnp.float32), block_size, axis=1)
    return jnp.transpose(lax.dynamic_slice_in_dim(flat_mask, position * rows_dev, rows_dev, 1))[
        :, :, None
    ]


def reduce_body(sigma_anc, anc_factor, diag_inverse, pattern):
    precise = lax.Precision.HIGHEST
    rows_dev, _, super_width = anc_factor.shape
    row_count = lax.axis_size("row")
    col_count = lax.axis_size("col")
    position = lax.axis_index("row") * col_count + lax.axis_index("col")
    device_total = row_count * col_count
    own_mask = own_row_mask(pattern, rows_dev, position, rows_dev * device_total)
    share = -(-super_width // device_total)
    masked_factor = anc_factor * own_mask
    flattened = masked_factor.reshape(rows_dev, -1)
    gathered = lax.all_gather(flattened, "row", axis=0, tiled=True)
    stacked = gathered.reshape(row_count, rows_dev, flattened.shape[1])
    turned = lax.all_to_all(stacked, "col", split_axis=0, concat_axis=1, tiled=True)
    column_block = turned.reshape(row_count * rows_dev, flattened.shape[1])
    summed_rows = lax.psum_scatter(
        jnp.dot(sigma_anc, column_block, precision=precise, preferred_element_type=jnp.float32),
        "col",
        scatter_dimension=0,
        tiled=True,
    )
    off_factor = -(summed_rows.reshape(masked_factor.shape) * own_mask)
    both_rows = jnp.concatenate([masked_factor, off_factor], axis=0)
    column_piece = lax.all_gather(diag_inverse, "row", axis=2, tiled=True)
    product = jnp.einsum("rsk,skj->rsj", both_rows, column_piece, precision=precise)
    own_rows = lax.dynamic_slice_in_dim(column_piece, position * share, share, 1)
    scaled = product[:rows_dev]
    sel_off = product[rows_dev:]
    diag_term = jnp.einsum("skj,skl->sjl", own_rows, own_rows, precision=precise)
    partial_value = diag_term - jnp.einsum("rsj,rsl->sjl", scaled, sel_off, precision=precise)
    sel_diag = lax.psum(partial_value, ("row", "col"))
    return (sel_off, sel_diag)


def swap(value, axis, bit):
    count = lax.axis_size(axis)
    return lax.ppermute(value, axis, [(i, i ^ bit) for i in range(count)])


def halves(value):
    high = value.astype(jnp.bfloat16)
    return high, (value - high.astype(jnp.float32)).astype(jnp.bfloat16)


ROWS_BY_COLUMNS = (((1,), (0,)), ((), ()))


def product3(left, right, dims):
    a = jnp.concatenate([left[0], left[0], left[1]], axis=1)
    b = jnp.concatenate([right[0], right[1], right[0]], axis=0)
    return lax.dot_general(a, b, dims, preferred_element_type=jnp.float32)


def unique_tiles(core, tile):
    base = core * (2 * tile)
    tiles = [(base, base), (base, base + tile), (base + tile, base + tile)]
    for i in range(2):
        tiles.append((base + i * tile, jnp.where(core == 0, 2 + i, 1 - i) * tile))
    return [(pl.multiple_of(i, tile), pl.multiple_of(j, tile)) for i, j in tiles]


def put_unique(out, extra, band, core, tile):
    base = core * (2 * tile)
    for n, (i, j) in enumerate(unique_tiles(core, tile)):
        at = pl.ds(n * tile, tile)
        value = band[pl.ds(pl.multiple_of(i - base, tile), tile), pl.ds(j, tile)]
        out[at, :] = value if extra is None else value + extra[at, :]


def split_kernel(cores, rows, mine, theirs):
    own_first = lax.axis_index("row") < cores
    first, second = rows[:, 0, :], rows[:, 1, :]
    mine[...] = jnp.where(own_first, first, second)
    theirs[...] = jnp.where(own_first, second, first)


def inverse_kernel(cores, own, partner, own_core, partner_core, *refs):
    high, low, gram_own, gram_other, band = refs
    row = lax.axis_index("row")
    share = own.shape[1]
    width = high.shape[0]
    tile = width // 4
    for step, value in enumerate((own, own_core, partner, partner_core)):
        place = pl.ds(pl.multiple_of((row ^ step) * share, share), share)
        high[:, place], low[:, place] = halves(value[...])
    core = lax.rem(row, cores)
    half = width // cores
    rows = pl.ds(pl.multiple_of(core * half, half), half)
    for who, out in ((core, gram_own), (1 - core, gram_other)):
        columns = pl.ds(pl.multiple_of(who * half, half), half)
        left = (high[rows, columns].T, low[rows, columns].T)
        band[...] = product3(left, (high[rows, :], low[rows, :]), ROWS_BY_COLUMNS)
        put_unique(out, None, band, who, tile)


def scale_kernel(ks, cores, cols, block_size, pattern_ref, high, low, *refs):
    pieces, out, split_high, split_low = refs[:-3], refs[-3], refs[-2], refs[-1]
    row, col = lax.axis_index("row"), lax.axis_index("col")
    supers, rows_dev, _ = pieces[0].shape
    for n, piece in enumerate(pieces):
        for p in range(supers):
            at = pl.ds((n * supers + p) * rows_dev, rows_dev)
            split_high[at, :], split_low[at, :] = halves(piece[p])
    scaled = product3(
        (split_high[...], split_low[...]), (high[...], low[...]), ROWS_BY_COLUMNS
    )
    present = pattern_ref[pl.ds(row // cores, 1), :].astype(jnp.float32)
    index = lax.broadcasted_iota(jnp.int32, (rows_dev, 1), 0)
    for n, k in enumerate(ks):
        for p in range(supers):
            start = ((row ^ (p * cores)) * cols + (col ^ k)) * rows_dev
            mask = jnp.zeros((rows_dev, 1), jnp.float32)
            for b in range(pattern_ref.shape[1]):
                inside = (index + start >= b * block_size) & (index + start < (b + 1) * block_size)
                mask = jnp.where(inside, present[:, b : b + 1], mask)
            first = (n * supers + p) * rows_dev
            out[n, p] = scaled[first : first + rows_dev] * mask


def prepare_kernel(cols, ks, *refs):
    sig = refs[:cols]
    partner = refs[cols : 2 * cols]
    groups = refs[2 * cols : 2 * cols + len(ks)]
    left_high, left_low, turned_high, turned_low, rows_high, rows_low = refs[2 * cols + len(ks) :]
    col = lax.axis_index("col")
    _, supers, rows_dev, _ = groups[0].shape
    block = sig[0].shape[0]
    for k in range(0, cols, 2):
        for n, source in enumerate((sig, partner)):
            at = (pl.ds(n * block, block), pl.ds(k * block, 2 * block))
            left_high[at], left_low[at] = halves(
                jnp.concatenate([source[k][...], source[k + 1][...]], axis=1)
            )
    for group, members in zip(groups, ks):
        for n, k in enumerate(members):
            for p in range(supers):
                at = pl.ds(pl.multiple_of(p * block + (col ^ k) * rows_dev, 16), rows_dev)
                rows_high[at, :], rows_low[at, :] = halves(group[n, p])
    turned_high[...] = rows_high[...].T
    turned_low[...] = rows_low[...].T


def product_kernel(cores, ks, gram_other, *refs):
    left_high, left_low, turned_high, turned_low = refs[:4]
    count = len(ks)
    groups, groups_core = refs[4 : 4 + count], refs[4 + count : 4 + 2 * count]
    sent, kept, away, y_high, y_low, right_high, right_low, band = refs[4 + 2 * count :]
    row, col = lax.axis_index("row"), lax.axis_index("col")
    _, supers, rows_dev, width = groups[0].shape
    block = y_high.shape[0] // supers
    tile = width // 4
    half = width // cores
    for c, source in enumerate((groups, groups_core)):
        for group, members in zip(source, ks):
            for n, k in enumerate(members):
                for p in range(supers):
                    which = (col ^ row) ^ (p * cores + c)
                    at = pl.multiple_of(which * block + (col ^ k) * rows_dev, 16)
                    at = pl.ds(at, rows_dev)
                    right_high[at, :], right_low[at, :] = halves(group[n, p])
    spread = product3(
        (left_high[...], left_low[...]), (right_high[...], right_low[...]), ROWS_BY_COLUMNS
    )
    y_high[...], y_low[...] = halves(spread)

    def rows_at(start):
        at = pl.ds(pl.multiple_of(start + col * rows_dev, 16), rows_dev)
        return y_high[at, :].astype(jnp.float32) + y_low[at, :].astype(jnp.float32)

    kept[...] = rows_at(0)
    sent[...] = rows_at(block)
    other = 1 - lax.rem(row, cores)
    at = pl.ds(pl.multiple_of(other * half, half), half)
    left = (turned_high[at, :], turned_low[at, :])
    band[...] = product3(left, (y_high[...], y_low[...]), ROWS_BY_COLUMNS)
    put_unique(away, gram_other, band, other, tile)


def own_kernel(cores, gram_own, turned_high, turned_low, y_high, y_low, out, band):
    core = lax.rem(lax.axis_index("row"), cores)
    half = band.shape[0]
    at = pl.ds(pl.multiple_of(core * half, half), half)
    left = (turned_high[at, :], turned_low[at, :])
    band[...] = product3(left, (y_high[...], y_low[...]), ROWS_BY_COLUMNS)
    put_unique(out, gram_own, band, core, out.shape[1])


def local_call(kernel, outs, scratch, args, flops, limit):
    in_specs = [pl.BlockSpec(memory_space=pltpu.VMEM)] * len(args)
    moved = sum(a.size * a.dtype.itemsize for a in list(args) + list(outs))
    return pl.pallas_call(
        kernel,
        out_shape=outs,
        in_specs=in_specs,
        out_specs=[pl.BlockSpec(memory_space=pltpu.VMEM)] * len(outs),
        scratch_shapes=scratch,
        cost_estimate=pl.CostEstimate(flops=flops, transcendentals=0, bytes_accessed=moved),
        compiler_params=pltpu.CompilerParams(vmem_limit_bytes=limit),
    )(*args)


def lay_out(tile, cores, specs, away, *refs):
    out_ref, turned, sems = refs[-3:]
    row, col = lax.axis_index("row"), lax.axis_index("col")
    index = (row // cores) ^ away
    copies = []

    def put(value, i, j):
        i, j = pl.multiple_of(i, tile), pl.multiple_of(j, tile)
        target = out_ref.at[index, pl.ds(i, tile), pl.ds(j, tile)]
        copies.append(pltpu.make_async_copy(value, target, sems.at[len(copies)]))
        copies[-1].start()

    mirrored = []
    for source, (flip, members) in zip(refs, specs):
        core = lax.rem(row, cores) ^ flip
        tiles = unique_tiles(core, tile)
        for n, member in enumerate(members):
            if member >= 0:
                i, j = tiles[member]
            else:
                which = lax.rem(col, 2) ^ (-1 - member)
                i = (core * 2 + which) * tile
                j = jnp.where(core == 0, 2 + which, 1 - which) * tile
            at = pl.ds(n * tile, tile)
            put(source.at[at, :], i, j)
            if member not in (0, 2):
                turned[len(mirrored)] = source[at, :].T
                mirrored.append((j, i))
    for n, (i, j) in enumerate(mirrored):
        put(turned.at[n], i, j)
    for copy in copies:
        copy.wait()


def place_square(supers, width, cores, away, parts, specs, target=None):
    tile = width // 4
    args = [*parts] + ([] if target is None else [target])
    members = [m for _, ms in specs for m in ms]
    mirrors = sum(m not in (0, 2) for m in members)
    return pl.pallas_call(
        functools.partial(lay_out, tile, cores, specs, away),
        out_shape=jax.ShapeDtypeStruct((supers, width, width), jnp.float32),
        in_specs=[pl.BlockSpec(memory_space=pltpu.VMEM)] * len(parts)
        + ([] if target is None else [pl.BlockSpec(memory_space=pl.ANY)]),
        out_specs=pl.BlockSpec(memory_space=pl.ANY),
        scratch_shapes=[
            pltpu.VMEM((max(mirrors, 1), tile, tile), jnp.float32),
            pltpu.SemaphoreType.DMA((len(members) + mirrors,)),
        ],
        input_output_aliases={} if target is None else {len(parts): 0},
        cost_estimate=pl.CostEstimate(
            flops=0, transcendentals=0, bytes_accessed=2 * 4 * width * width
        ),
        compiler_params=pltpu.CompilerParams(vmem_limit_bytes=8 * 4 * width * width),
        name="lk",
    )(*args)


def join_rows(mask_ref, first_ref, second_ref, out_ref):
    out_ref[:, 0, :] = -(first_ref[...] * mask_ref[:, 0:1])
    out_ref[:, 1, :] = -(second_ref[...] * mask_ref[:, 1:2])


def gather_body(sigma_anc, anc_factor, diag_inverse, pattern):
    high = lax.Precision.HIGH
    rows_dev, supers, width = anc_factor.shape
    row_count = lax.axis_size("row")
    col_count = lax.axis_size("col")
    cores = row_count // supers
    row = lax.axis_index("row")
    col = lax.axis_index("col")
    plane = row // cores
    first = plane == 0
    block_rows = rows_dev * col_count
    total_rows = block_rows * row_count
    tile = width // 4
    half = width // cores

    def other_plane(value):
        return swap(value, "row", cores)

    def other_core(value):
        return swap(value, "row", 1)

    def pick(value, index):
        return lax.dynamic_index_in_dim(value, index, 0, keepdims=False)

    def along_col(value, partner):
        return swap(value, "col", partner)

    mine, theirs = local_call(
        functools.partial(split_kernel, cores),
        [jax.ShapeDtypeStruct((rows_dev, width), jnp.float32)] * 2,
        [],
        [anc_factor],
        0,
        8 * 4 * width * width,
    )
    partner = other_plane(theirs)
    rows_sent = jnp.stack([mine, partner])
    far = along_col(rows_sent, 2)
    near = along_col(rows_sent, 1)
    pieces = [rows_sent, near, far, along_col(far, 1)]
    flat_mask = jnp.repeat(pattern.astype(jnp.float32), total_rows // pattern.shape[1], axis=1)
    own_mask = jnp.transpose(
        lax.dynamic_slice_in_dim(flat_mask, row * block_rows + col * rows_dev, rows_dev, 1)
    )

    sig = [sigma_anc, along_col(sigma_anc, 1), along_col(sigma_anc, 2)]
    sig.append(along_col(sig[2], 1))
    sig_partner = [other_plane(sig[k]) for k in range(col_count)]

    d_own = pick(diag_inverse, plane)
    d_sent = pick(diag_inverse, 1 - plane)
    d_partner = other_plane(d_sent)
    d_own_core = other_core(d_own)
    d_partner_core = other_core(d_partner)

    def shaped(shape, dtype=jnp.float32):
        return jax.ShapeDtypeStruct(shape, dtype)

    wide = shaped((width, width), jnp.bfloat16)
    unique = shaped((5 * tile, tile))
    square_bytes = 4 * width * width
    band = pltpu.VMEM((half, width), jnp.float32)
    high, low, gram_own, gram_other = local_call(
        functools.partial(inverse_kernel, cores),
        [wide, wide, unique, unique],
        [band],
        [d_own, d_partner, d_own_core, d_partner_core],
        6 * half * half * width,
        8 * square_bytes,
    )

    ks = ((0, 2), (1,), (3,))

    def scale(members):
        count = len(members) * supers * rows_dev
        return local_call(
            functools.partial(
                scale_kernel, members, cores, col_count, total_rows // pattern.shape[1]
            ),
            [shaped((len(members), supers, rows_dev, width))],
            [pltpu.VMEM((count, width), jnp.bfloat16)] * 2,
            [pattern, high, low] + [pieces[k] for k in members],
            6 * count * width * width,
            8 * square_bytes,
        )[0]

    groups = [scale(members) for members in ks]
    groups_core = [other_core(group) for group in groups]
    x_rows = supers * block_rows
    left_high, left_low, turned_high, turned_low = local_call(
        functools.partial(prepare_kernel, col_count, ks),
        [shaped((x_rows, total_rows), jnp.bfloat16)] * 2
        + [shaped((width, x_rows), jnp.bfloat16)] * 2,
        [pltpu.VMEM((x_rows, width), jnp.bfloat16)] * 2,
        [*sig, *sig_partner, *groups],
        x_rows * total_rows,
        8 * square_bytes,
    )
    split = shaped((x_rows, width), jnp.bfloat16)
    rows_out = shaped((rows_dev, width))
    sent, kept, away, y_high, y_low = local_call(
        functools.partial(product_kernel, cores, ks),
        [rows_out, rows_out, unique, split, split],
        [pltpu.VMEM((total_rows, width), jnp.bfloat16)] * 2 + [band],
        [gram_other, left_high, left_low, turned_high, turned_low, *groups, *groups_core],
        6 * x_rows * total_rows * width,
        16 * square_bytes,
    )

    got = other_plane(sent)
    sel_off = pl.pallas_call(
        join_rows,
        out_shape=jax.ShapeDtypeStruct(anc_factor.shape, jnp.float32),
        cost_estimate=pl.CostEstimate(
            flops=0, transcendentals=0, bytes_accessed=8 * rows_dev * supers * width
        ),
        compiler_params=pltpu.CompilerParams(vmem_limit_bytes=8 * 4 * width * width),
        name="jk",
    )(own_mask, jnp.where(first, kept, got), jnp.where(first, got, kept))

    received = other_core(away)
    (own_blocks,) = local_call(
        functools.partial(own_kernel, cores),
        [unique],
        [band],
        [gram_own, turned_high, turned_low, y_high, y_low],
        6 * half * x_rows * width,
        8 * square_bytes,
    )
    finished = own_blocks + received
    moved = lax.dynamic_slice_in_dim(finished, (3 + col % 2) * tile, tile, 0)
    far_tile = other_plane(moved)
    far_finished = other_plane(finished[: 3 * tile])
    finished_core = other_core(finished)
    next_tile = swap(far_tile, "col", 1)
    tile_core = other_core(far_tile)
    next_core = other_core(next_tile)
    far_core = other_core(far_finished)
    every, most = (0, 1, 2, 3, 4), (0, 1, 2)
    square = place_square(
        supers, width, cores, 0, [finished, finished_core], ((0, every), (1, every))
    )
    square = place_square(
        supers, width, cores, 1, [far_tile, tile_core], ((0, (-1,)), (1, (-1,))), square
    )
    square = place_square(supers, width, cores, 1, [far_finished], ((0, most),), square)
    sel_diag = place_square(
        supers,
        width,
        cores,
        1,
        [far_core, next_tile, next_core],
        ((1, most), (0, (-2,)), (1, (-2,))),
        square,
    )
    return (sel_off, sel_diag)


def gather_fits(row_count, col_count, supers):
    return row_count == 2 * supers == 4 and col_count == 4


def body(sigma_anc, anc_factor, diag_inverse, pattern):
    supers = anc_factor.shape[1]
    if gather_fits(lax.axis_size("row"), lax.axis_size("col"), supers):
        return gather_body(sigma_anc, anc_factor, diag_inverse, pattern)
    return reduce_body(sigma_anc, anc_factor, diag_inverse, pattern)


def solution(mesh):
    return jax.shard_map(
        body,
        mesh=mesh,
        in_specs=(
            P(("grp", "row"), "col"),
            P(("grp", "row", "col"), None, None),
            P("grp", None, "row"),
            P(),
        ),
        out_specs=(P(("grp", "row", "col"), None, None), P("grp", None, None)),
        check_vma=False,
    )
```
